32 devices in a mesh: context: 16 (over z, y, core), tensor: 2 (over x).
Axes of the slice: x: 2, y: 2, z: 4, core: 2. Of those that a mesh axis runs over, the one named last changes fastest.
Arguments:
- queries: bfloat16 [4096, 2048], P(('context', 'tensor')), may hold values from -6 to 6
- key_rows: bfloat16 [4096, 2048], P(('context', 'tensor')), may hold values from -6 to 6
- value_rows: bfloat16 [4096, 2048], P(('context', 'tensor')), may hold values from -6 to 6
- grad_output: bfloat16 [4096, 2048], P(('context', 'tensor')), may hold values from -6 to 6
Outputs:
- attended: bfloat16 [4096, 2048], P(('context', 'tensor'))
- grad_queries: bfloat16 [4096, 2048], P(('context', 'tensor'))
- grad_keys: bfloat16 [4096, 2048], P(('context', 'tensor'))
- grad_values: bfloat16 [4096, 2048], P(('context', 'tensor'))
The draws below stay inside these ranges and needn't reach their ends.
All inputs are finite; a program needn't handle non-finite values.
Results may differ from the reference program's by a relative error of at most 0.007.
Values may be sent and summed in bfloat16 or wider, within the bound.
No kernel may reach another device: no remote copies, remote signals or barrier semaphores. Data moves between devices by JAX's collectives and lax.ppermute only.
A program may use at most 64 MiB of HBM per device.

```python
import jax
import jax.numpy as jnp
from jax import lax

H = 16
DH = 128
TOK_DEV = 128
TOKENS = 4096


def levels(own_key, shape, cuts, smallest, high):
    gain, own = 1.0, jax.random.fold_in(own_key, 6)
    for axis_at, parts in cuts:
        heights = jnp.exp(jax.random.uniform(jax.random.fold_in(own, axis_at), (parts,), jnp.float32, smallest / len(cuts), high / len(cuts)))
        gain = gain * jnp.repeat(heights, shape[axis_at] // parts).reshape([-1 if axis == axis_at else 1 for axis in range(len(shape))])
    return gain


def gaussian(own_key, shape, width, reach, shards=(), held_as=jnp.bfloat16):
    drawn = jax.random.normal(own_key, shape, jnp.float32) * width
    if len(shards) > 0:
        drawn = levels(own_key, shape, shards, -0.22, 0.18) * drawn
    return jnp.clip(drawn, min=-reach, max=reach).astype(held_as)


def setup_inputs(seed: int = 0) -> dict:
    arg_keys = jax.random.split(jax.random.key(seed), 5)
    return {
        "queries": gaussian(arg_keys[0], (TOKENS, H * DH), 1.0, 6.0, ((0, 32),)),
        "key_rows": gaussian(arg_keys[1], (TOKENS, H * DH), 1.0, 6.0, ((0, 32),)),
        "value_rows": gaussian(arg_keys[2], (TOKENS, H * DH), 1.0, 6.0, ((0, 32),)),
        "grad_output": gaussian(arg_keys[3], (TOKENS, H * DH), 1.0, 6.0, ((0, 32),)),
    }


eps = 1e-06

def reference(queries, key_rows, value_rows, grad_output):
    block_rows = TOK_DEV
    blocks_count = TOKENS // block_rows
    precise = lax.Precision.HIGHEST

    def to_blocks(source):
        return source.reshape(blocks_count, block_rows, H, DH)
    query_all = to_blocks(queries)
    key_all = to_blocks(key_rows)
    value_all = to_blocks(value_rows)
    positions = jnp.arange(block_rows, dtype=jnp.int32)
    causal = positions[:, None] >= positions[None, :]
    empty_state = jnp.zeros((H, DH, DH), jnp.float32)

    def forward(state_now, inputs_now):
        query_f = inputs_now[0].astype(jnp.float32)
        key_f = inputs_now[1].astype(jnp.float32)
        value_f = inputs_now[2].astype(jnp.float32)
        scores = jnp.einsum('ihd,jhd->hij', query_f, key_f)
        weights = jnp.where(causal[None], scores, 0.0).astype(jnp.bfloat16)
        attn_out = jnp.einsum('hij,jhd->ihd', weights.astype(jnp.float32), value_f)
        attn_out = attn_out + jnp.einsum('ihd,hde->ihe', query_f, state_now, precision=precise)
        new_state = state_now + jnp.einsum('jhd,jhe->hde', key_f, value_f)
        return (new_state, (attn_out, state_now))
    _, (attn, prefixes) = lax.scan(forward, empty_state, (query_all, key_all, value_all))
    root_mean = jnp.sqrt(lax.optimization_barrier(jnp.mean(attn * attn, axis=-1, keepdims=True)) + eps)
    normed = attn / root_mean
    cotangent = to_blocks(grad_output).astype(jnp.float32)
    d_attn = ((cotangent - normed * lax.optimization_barrier(jnp.mean(cotangent * normed, axis=-1, keepdims=True))) / root_mean).astype(jnp.bfloat16)

    def backward(suffix, inputs_now):
        query_f = inputs_now[0].astype(jnp.float32)
        key_f = inputs_now[1].astype(jnp.float32)
        value_f = inputs_now[2].astype(jnp.float32)
        grad_f = inputs_now[3].astype(jnp.float32)
        state_now = inputs_now[4]
        scores = jnp.einsum('ihd,jhd->hij', query_f, key_f)
        weights = jnp.where(causal[None], scores, 0.0).astype(jnp.bfloat16).astype(jnp.float32)
        d_scores = jnp.einsum('ihd,jhd->hij', grad_f, value_f)
        d_weights = jnp.where(causal[None], d_scores, 0.0).astype(jnp.bfloat16).astype(jnp.float32)
        grad_query = jnp.einsum('hij,jhd->ihd', d_weights, key_f) + jnp.einsum('ihe,hde->ihd', grad_f, state_now, precision=precise)
        grad_key = jnp.einsum('hij,ihd->jhd', d_weights, query_f) + jnp.einsum('jhe,hde->jhd', value_f, suffix, precision=precise)
        grad_value = jnp.einsum('hij,ihd->jhd', weights, grad_f) + jnp.einsum('jhd,hde->jhe', key_f, suffix, precision=precise)
        new_suffix = suffix + jnp.einsum('ihd,ihe->hde', query_f, grad_f)
        return (new_suffix, (grad_query, grad_key, grad_value))
    _, (grad_query, grad_key, grad_value) = lax.scan(backward, empty_state, (query_all, key_all, value_all, d_attn, prefixes), reverse=True)

    def flatten(source):
        return source.reshape(TOKENS, H * DH).astype(jnp.bfloat16)
    return (flatten(normed), flatten(grad_query), flatten(grad_key), flatten(grad_value))
```

```python
import functools

import jax
import jax.numpy as jnp
from jax import lax
from jax.experimental import pallas as pl
from jax.experimental.pallas import tpu as pltpu
from jax.sharding import PartitionSpec as P

DH = 128
AXES = ("context", "tensor")
MAX_OWNERS = 8

eps = 1e-06

F32 = jnp.float32
BF16 = jnp.bfloat16


def dot(a, b, contract):
    return lax.dot_general(a, b, ((contract[:1], contract[1:]), ((), ())), preferred_element_type=F32)


def vmem(count):
    return [pl.BlockSpec(memory_space=pltpu.VMEM)] * count


def params():
    return pltpu.CompilerParams(vmem_limit_bytes=24 * 1024 * 1024)


def cost(flops, moved):
    return pl.CostEstimate(flops=flops, bytes_accessed=moved, transcendentals=0)


def place(owners):
    return lax.rem(lax.axis_index(AXES[0]) * lax.axis_size(AXES[1]) + lax.axis_index(AXES[1]), owners)


def columns(p, m, j, share):
    return pl.ds(pl.multiple_of((jnp.bitwise_xor(p, m) * share + j) * DH, DH), DH)


def causal_mask(rows):
    return lax.broadcasted_iota(jnp.int32, (rows, rows), 0) >= lax.broadcasted_iota(jnp.int32, (rows, rows), 1)


def states_kernel(owners, share, left, right, *outs):
    p = place(owners)
    for m in range(owners):
        for j in range(share):
            at = columns(p, m, j, share)
            outs[m][j] = dot(left[:, at], right[:, at], (0, 0)).astype(BF16)


def prefix_kernel(owners, reverse, count, *refs):
    keep = refs[0]
    parts = refs[1 : 1 + owners]
    others = refs[1 + owners : 1 + owners + count]
    outs = refs[1 + owners + count :]
    p = place(owners)
    for j in range(parts[0].shape[0]):
        base = jnp.zeros(parts[0].shape[1:], F32)
        for k in range(count):
            base = base + jnp.where(keep[k] > 0, others[k][j].astype(F32), 0.0)
        total = [part[j].astype(F32) for part in parts]
        before = [base] * owners
        bit = 1
        while bit < owners:
            mine = jnp.bitwise_and(p, bit) > 0
            for m in range(owners):
                taken = (mine == (m & bit > 0)) if reverse else (mine != (m & bit > 0))
                before[m] = before[m] + jnp.where(taken, total[m ^ bit], 0.0)
            total = [total[m] + total[m ^ bit] for m in range(owners)]
            bit *= 2
        for m in range(owners):
            outs[m][j] = before[m].astype(BF16)


def within_kernel(heads, q, k, v, weights, attn):
    causal = causal_mask(q.shape[0])
    for h in range(heads):
        at = slice(h * DH, (h + 1) * DH)
        w = jnp.where(causal, dot(q[:, at], k[:, at], (1, 1)), 0.0).astype(BF16)
        weights[h] = w
        attn[:, at] = dot(w, v[:, at], (1, 0))


def forward_kernel(owners, share, q, g, within, *refs):
    states = refs[:owners]
    attended, d_attn = refs[owners : owners + 2]
    outs = refs[owners + 2 :]
    p = place(owners)
    for m in range(owners):
        for j in range(share):
            at = columns(p, m, j, share)
            query = q[:, at]
            attn = within[:, at] + dot(query, states[m][j], (1, 0))
            root = jnp.sqrt(jnp.mean(attn * attn, axis=1, keepdims=True) + eps)
            inverse = 1.0 / root
            normed = attn * inverse
            attended[:, at] = normed.astype(BF16)
            cotangent = g[:, at].astype(F32)
            inner = jnp.mean(cotangent * normed, axis=1, keepdims=True)
            d = ((cotangent - normed * inner) * inverse).astype(BF16)
            d_attn[:, at] = d
            outs[m][j] = dot(query, d, (0, 0)).astype(BF16)


def middle_kernel(owners, share, q, k, v, d_attn, weights, *refs):
    states = refs[:owners]
    d_query, d_key, d_value = refs[owners:]
    p = place(owners)
    causal = causal_mask(q.shape[0])
    for m in range(owners):
        for j in range(share):
            at = columns(p, m, j, share)
            d = d_attn[:, at]
            dw = jnp.where(causal, dot(d, v[:, at], (1, 1)), 0.0).astype(BF16)
            d_query[:, at] = (dot(dw, k[:, at], (1, 0)) + dot(d, states[m][j], (1, 1))).astype(BF16)
            d_key[:, at] = dot(dw, q[:, at], (0, 0))
            d_value[:, at] = dot(weights[jnp.bitwise_xor(p, m) * share + j], d, (0, 0))


def final_kernel(owners, share, k, v, key_part, value_part, *refs):
    states = refs[:owners]
    d_key, d_value = refs[owners:]
    p = place(owners)
    for m in range(owners):
        for j in range(share):
            at = columns(p, m, j, share)
            suffix = states[m][j]
            d_key[:, at] = (key_part[:, at] + dot(v[:, at], suffix, (1, 1))).astype(BF16)
            d_value[:, at] = (value_part[:, at] + dot(k[:, at], suffix, (1, 0))).astype(BF16)


def digits(planes):
    found, stride = [], 1
    while stride < planes:
        rest = planes // stride
        radix = next(r for r in (4, 2, 3, 5, 7, rest) if rest % r == 0)
        found.append((stride, radix))
        stride *= radix
    return found


def scan(parts, owners, planes, share, reverse):
    count = owners * planes
    here = lax.axis_index(AXES[0]) * lax.axis_size(AXES[1]) + lax.axis_index(AXES[1])
    order = sorted(range(1, owners), key=lambda m: (-bin(m).count("1"), -m))

    def exchange(items):
        got = list(items)
        for m in order:
            got[m] = lax.ppermute(items[m], AXES, [(i, i ^ m) for i in range(count)])
        return got

    mine = exchange(parts)
    plane = here // owners
    total = sum(part.astype(F32) for part in mine).astype(BF16)
    others, keep = [], []
    levels = digits(planes)
    for level, (stride, radix) in enumerate(levels):
        digit = (plane // stride) % radix
        received = []
        for step in range(1, radix):

            def target(i):
                own = (i // owners // stride) % radix
                new = (own - step) % radix if reverse else (own + step) % radix
                return i + (new - own) * stride * owners

            received.append(lax.ppermute(total, AXES, [(i, target(i)) for i in range(count)]))
            keep.append(digit + step < radix if reverse else digit >= step)
        others += received
        if level + 1 < len(levels):
            total = (total.astype(F32) + sum(part.astype(F32) for part in received)).astype(BF16)
    kept = jnp.stack([flag.astype(jnp.int32) for flag in keep] or [jnp.int32(0)])
    shape = jax.ShapeDtypeStruct(parts[0].shape, BF16)
    moved = (2 * owners + len(others)) * shape.size * 2
    back = pl.pallas_call(
        functools.partial(prefix_kernel, owners, reverse, len(others)),
        out_shape=[shape] * owners,
        in_specs=[pl.BlockSpec(memory_space=pltpu.SMEM)] + vmem(owners + len(others)),
        out_specs=vmem(owners),
        compiler_params=params(),
        cost_estimate=cost(0, moved),
        name="suffixes" if reverse else "prefixes",
    )(kept, *mine, *others)
    return exchange(back)


def body(queries, key_rows, value_rows, grad_output):
    rows, width = queries.shape
    heads = width // DH
    count = lax.axis_size(AXES[0]) * lax.axis_size(AXES[1])
    owners = 1
    while owners < MAX_OWNERS and count % (2 * owners) == 0 and heads % (2 * owners) == 0:
        owners *= 2
    share, planes = heads // owners, count // owners
    share_shape = jax.ShapeDtypeStruct((share, DH, DH), BF16)
    flat = jax.ShapeDtypeStruct((rows, width), BF16)
    wide = jax.ShapeDtypeStruct((rows, width), F32)
    one = 2 * rows * width * DH
    size = rows * width * 2

    states = pl.pallas_call(
        functools.partial(states_kernel, owners, share),
        out_shape=[share_shape] * owners,
        in_specs=vmem(2),
        out_specs=vmem(owners),
        compiler_params=params(),
        cost_estimate=cost(one, 3 * size),
        name="states",
    )(key_rows, value_rows)
    weights, within = pl.pallas_call(
        functools.partial(within_kernel, heads),
        out_shape=[jax.ShapeDtypeStruct((heads, rows, rows), BF16), wide],
        in_specs=vmem(3),
        out_specs=vmem(2),
        compiler_params=params(),
        cost_estimate=cost(2 * one, 6 * size),
        name="within",
    )(queries, key_rows, value_rows)
    before = scan(states, owners, planes, share, False)
    attended, d_attn, *grad_states = pl.pallas_call(
        functools.partial(forward_kernel, owners, share),
        out_shape=[flat, flat] + [share_shape] * owners,
        in_specs=vmem(3 + owners),
        out_specs=vmem(2 + owners),
        compiler_params=params(),
        cost_estimate=cost(2 * one, 8 * size),
        name="forward",
    )(queries, grad_output, within, *before)
    grad_queries, key_part, value_part = pl.pallas_call(
        functools.partial(middle_kernel, owners, share),
        out_shape=[flat, wide, wide],
        in_specs=vmem(5 + owners),
        out_specs=vmem(3),
        compiler_params=params(),
        cost_estimate=cost(5 * one, 11 * size),
        name="middle",
    )(queries, key_rows, value_rows, d_attn, weights, *before)
    after = scan(grad_states, owners, planes, share, True)
    grad_keys, grad_values = pl.pallas_call(
        functools.partial(final_kernel, owners, share),
        out_shape=[flat, flat],
        in_specs=vmem(4 + owners),
        out_specs=vmem(2),
        compiler_params=params(),
        cost_estimate=cost(2 * one, 9 * size),
        name="final",
    )(key_rows, value_rows, key_part, value_part, *after)
    return (attended, grad_queries, grad_keys, grad_values)


def solution(mesh):
    spec = P(AXES, None)
    return jax.shard_map(body, mesh=mesh, in_specs=(spec,) * 4, out_specs=(spec,) * 4, check_vma=False)
```

```python
import functools

import jax
import jax.numpy as jnp
from jax import lax
from jax.experimental import pallas as pl
from jax.experimental.pallas import tpu as pltpu
from jax.sharding import PartitionSpec as P

DH = 128
AXES = ("context", "tensor")
PLANE = 8
GROUP = 4
OWNERS = 4

eps = 1e-06

F32 = jnp.float32
BF16 = jnp.bfloat16


def dot(a, b, contract):
    return lax.dot_general(a, b, ((contract[:1], contract[1:]), ((), ())), preferred_element_type=F32)


def pair_bit():
    pair = lax.axis_size(AXES[1]) if lax.axis_size(AXES[1]) < GROUP else 1
    return pair, (GROUP - 1) ^ pair, GROUP


def here():
    return lax.axis_index(AXES[0]) * lax.axis_size(AXES[1]) + lax.axis_index(AXES[1])


def has(bit):
    return jnp.bitwise_and(here(), bit) > 0


def owner_xor(r):
    _, near, far = pair_bit()
    return (near if r & 1 else 0) ^ (far if r & 2 else 0)


def owner():
    _, near, far = pair_bit()
    return has(near).astype(jnp.int32) + 2 * has(far).astype(jnp.int32)


def swap(x, bits):
    count = lax.axis_size(AXES[0]) * lax.axis_size(AXES[1])
    return lax.ppermute(x, AXES, [(i, i ^ bits) for i in range(count)])


def call(kernel, name, inputs, outs, flops=0, hbm_in=False, hbm_out=False, scratch=(), grant=16):
    space_in = pl.BlockSpec(memory_space=pl.ANY if hbm_in else pltpu.VMEM)
    space_out = pl.BlockSpec(memory_space=pl.ANY if hbm_out else pltpu.VMEM)
    moved = sum(a.size * a.dtype.itemsize for a in list(inputs) + list(outs))
    return pl.pallas_call(
        kernel,
        out_shape=list(outs),
        in_specs=[space_in] * len(inputs),
        out_specs=[space_out] * len(outs),
        scratch_shapes=list(scratch),
        compiler_params=pltpu.CompilerParams(vmem_limit_bytes=grant * 1024 * 1024),
        cost_estimate=pl.CostEstimate(flops=flops, bytes_accessed=moved, transcendentals=0),
        name=name,
    )(*inputs)


def share_columns(r, j, share):
    head = jnp.bitwise_xor(owner(), r) * share + j
    return head, pl.ds(pl.multiple_of(head * DH, DH), DH)


def causal_mask(rows):
    return lax.broadcasted_iota(jnp.int32, (rows, rows), 0) >= lax.broadcasted_iota(jnp.int32, (rows, rows), 1)


def split_kernel(a, b, own, other, sems):
    half = own.shape[2]
    mine = has(pair_bit()[0]).astype(jnp.int32)
    copies = []
    for n, source in enumerate((a, b)):
        for k, target in enumerate((other, own)):
            at = pl.ds(pl.multiple_of((mine if k else 1 - mine) * half, half), half)
            copies.append(pltpu.make_async_copy(source.at[:, at], target.at[n], sems.at[n, k]))
    for copy in copies:
        copy.start()
    for copy in copies:
        copy.wait()


def join_kernel(own_a, other_a, own_b, other_b, a, b, sems):
    half = own_a.shape[1]
    mine = has(pair_bit()[0]).astype(jnp.int32)
    copies = []
    for n, (own, other, target) in enumerate(((own_a, other_a, a), (own_b, other_b, b))):
        for k, source in enumerate((other, own)):
            at = pl.ds(pl.multiple_of((mine if k else 1 - mine) * half, half), half)
            copies.append(pltpu.make_async_copy(source, target.at[:, at], sems.at[n, k]))
    for copy in copies:
        copy.start()
    for copy in copies:
        copy.wait()


def states_kernel(share, own, other, *outs):
    sums, every = outs[:OWNERS], outs[OWNERS]
    for r in range(OWNERS):
        for j in range(share):
            head, at = share_columns(r, j, share)
            first = dot(own[0, :, at], own[1, :, at], (0, 0))
            second = dot(other[0, :, at], other[1, :, at], (0, 0))
            every[0, head] = first.astype(BF16)
            every[1, head] = second.astype(BF16)
            sums[r][j] = (first + second).astype(BF16)


def sum_kernel(*refs):
    for j in range(refs[0].shape[0]):
        refs[-1][j] = sum(ref[j].astype(F32) for ref in refs[:-1]).astype(BF16)


def base_kernel(reverse, levels, *refs):
    steps = [(stride, radix, step) for stride, radix in levels for step in range(1, radix)]
    count = len(steps)
    parts, others, (mine, across) = refs[:OWNERS], refs[OWNERS : OWNERS + count], refs[OWNERS + count :]
    late = has(pair_bit()[2])
    plane = here() // PLANE
    for j in range(mine.shape[0]):
        base = jnp.zeros(mine.shape[1:], F32)
        for other, (stride, radix, step) in zip(others, steps):
            digit = lax.rem(plane // stride, radix)
            keep = digit + step < radix if reverse else digit >= step
            base = base + jnp.where(keep, other[j].astype(F32), 0.0)
        same = parts[0][j].astype(F32) + parts[1][j].astype(F32)
        far = parts[2][j].astype(F32) + parts[3][j].astype(F32)
        counts_far = jnp.logical_not(late) if reverse else late
        mine[j] = (base + jnp.where(counts_far, far, 0.0)).astype(BF16)
        across[j] = (base + jnp.where(counts_far, 0.0, same)).astype(BF16)


def group_states(reverse, head, base, every, direct):
    pair, near, _ = pair_bit()
    place = jnp.bitwise_and(here(), GROUP - 1)
    sources = [(0, every[0, head]), (pair, every[1, head]), (near, direct[0, head]), (near ^ pair, direct[1, head])]
    found = []
    for target in (0, pair):
        to = jnp.bitwise_xor(place, target)
        total = base.astype(F32)
        for mask, state in sources:
            if mask != target:
                source = jnp.bitwise_xor(place, mask)
                taken = source > to if reverse else source < to
                total = total + jnp.where(taken, state.astype(F32), 0.0)
        found.append(total.astype(BF16))
    return found


def within_kernel(heads, qg_own, qg_other, kv_own, kv_other, weights, attn):
    causal = causal_mask(qg_own.shape[1])
    for n, (qg, kv) in enumerate(((qg_own, kv_own), (qg_other, kv_other))):
        for h in range(heads):
            at = slice(h * DH, (h + 1) * DH)
            w = jnp.where(causal, dot(qg[0, :, at], kv[0, :, at], (1, 1)), 0.0).astype(BF16)
            weights[n, h] = w
            attn[n, :, at] = dot(w, kv[1, :, at], (1, 0))


def forward_kernel(share, qg_own, qg_other, within, *refs):
    bases, (every, direct), refs = refs[:OWNERS], refs[OWNERS : OWNERS + 2], refs[OWNERS + 2 :]
    att_own, att_other, d_attn, states, grad_every = refs[:5]
    grad_sums = refs[5:]
    for r in range(OWNERS):
        for j in range(share):
            head, at = share_columns(r, j, share)
            before = group_states(False, head, bases[r][j], every, direct)
            total = 0.0
            for n, (qg, out) in enumerate(((qg_own, att_own), (qg_other, att_other))):
                states[n, head] = before[n]
                query = qg[0, :, at]
                attn = within[n, :, at] + dot(query, before[n], (1, 0))
                inverse = 1.0 / jnp.sqrt(jnp.mean(attn * attn, axis=1, keepdims=True) + eps)
                normed = attn * inverse
                out[:, at] = normed.astype(BF16)
                cotangent = qg[1, :, at].astype(F32)
                inner = jnp.mean(cotangent * normed, axis=1, keepdims=True)
                d = ((cotangent - normed * inner) * inverse).astype(BF16)
                d_attn[n, :, at] = d
                grad = dot(query, d, (0, 0))
                grad_every[n, head] = grad.astype(BF16)
                total = total + grad
            grad_sums[r][j] = total.astype(BF16)


def middle_kernel(heads, qg_own, qg_other, kv_own, kv_other, d_attn, weights, states, *outs):
    dq_own, dq_other, key_part, value_part = outs
    causal = causal_mask(qg_own.shape[1])
    for n, (qg, kv, dq) in enumerate(((qg_own, kv_own, dq_own), (qg_other, kv_other, dq_other))):
        for h in range(heads):
            at = slice(h * DH, (h + 1) * DH)
            d = d_attn[n, :, at]
            dw = jnp.where(causal, dot(d, kv[1, :, at], (1, 1)), 0.0).astype(BF16)
            dq[:, at] = (dot(dw, kv[0, :, at], (1, 0)) + dot(d, states[n, h], (1, 1))).astype(BF16)
            key_part[n, :, at] = dot(dw, qg[0, :, at], (0, 0))
            value_part[n, :, at] = dot(weights[n, h], d, (0, 0))


def final_kernel(share, kv_own, kv_other, key_part, value_part, *refs):
    bases, (every, direct), outs = refs[:OWNERS], refs[OWNERS : OWNERS + 2], refs[OWNERS + 2 :]
    for r in range(OWNERS):
        for j in range(share):
            head, at = share_columns(r, j, share)
            after = group_states(True, head, bases[r][j], every, direct)
            for n, kv in enumerate((kv_own, kv_other)):
                d_key, d_value = outs[2 * n : 2 * n + 2]
                d_key[:, at] = (key_part[n, :, at] + dot(kv[1, :, at], after[n], (1, 1))).astype(BF16)
                d_value[:, at] = (value_part[n, :, at] + dot(kv[0, :, at], after[n], (1, 0))).astype(BF16)


def digits(planes):
    found, stride = [], 1
    while stride < planes:
        rest = planes // stride
        radix = next(r for r in (4, 2, 3, 5, 7, rest) if rest % r == 0)
        found.append((stride, radix))
        stride *= radix
    return found


def scan(sums, every, reverse, work, later):
    count = lax.axis_size(AXES[0]) * lax.axis_size(AXES[1])
    _, near, _ = pair_bit()
    received = [sums[0]] + [None] * (OWNERS - 1)
    for r in (3, 2, 1):
        received[r] = swap(sums[r], owner_xor(r))
    shape = jax.ShapeDtypeStruct(sums[0].shape, BF16)
    (total,) = call(sum_kernel, "total", received, [shape], grant=4)
    total, every, later = lax.optimization_barrier((total, every, later))
    levels = digits(count // PLANE)
    others = []
    for level, (stride, radix) in enumerate(levels):
        got = []
        for step in range(1, radix):

            def target(i):
                own = (i // PLANE // stride) % radix
                new = (own - step) % radix if reverse else (own + step) % radix
                return i + (new - own) * stride * PLANE

            got.append(lax.ppermute(total, AXES, [(i, target(i)) for i in range(count)]))
        others += got
        if level + 1 < len(levels):
            (total,) = call(sum_kernel, "total", [total, *got], [shape], grant=4)
    direct = swap(every, near)
    done = work(*later)
    others, done = lax.optimization_barrier((others, done))
    mine, across = call(
        functools.partial(base_kernel, reverse, levels),
        "suffixes" if reverse else "prefixes",
        [*received, *others],
        [shape] * 2,
        grant=4,
    )
    bases = [mine] + [None] * (OWNERS - 1)
    for r in (3, 2, 1):
        bases[r] = swap(across if r & 2 else mine, owner_xor(r))
    return bases, direct, done


def body(queries, key_rows, value_rows, grad_output):
    rows, width = queries.shape
    half = width // 2
    heads = half // DH
    share = heads // OWNERS
    count = lax.axis_size(AXES[0]) * lax.axis_size(AXES[1])
    assert count % PLANE == 0 and heads % OWNERS == 0
    pair = pair_bit()[0]
    one = 4 * rows * half * DH
    of = jax.ShapeDtypeStruct
    flat, flat_two, wide = of((rows, half), BF16), of((2, rows, half), BF16), of((2, rows, half), F32)
    full = of((rows, width), BF16)
    sums_shape, every_shape = [of((share, DH, DH), BF16)] * OWNERS, of((2, heads, DH, DH), BF16)
    sems = [pltpu.SemaphoreType.DMA((2, 2))]

    kv_own, kv_send = call(split_kernel, "split", [key_rows, value_rows], [flat_two] * 2, hbm_in=True, scratch=sems)
    kv_other = swap(kv_send, pair)
    *sums, every = call(
        functools.partial(states_kernel, share), "states", [kv_own, kv_other], sums_shape + [every_shape], one
    )
    queries, grad_output, *sums = lax.optimization_barrier((queries, grad_output, *sums))
    qg_own, qg_send = call(split_kernel, "split", [queries, grad_output], [flat_two] * 2, hbm_in=True, scratch=sems)
    qg_other = swap(qg_send, pair)

    def within_work(*operands):
        return call(
            functools.partial(within_kernel, heads),
            "within",
            operands,
            [of((2, heads, rows, rows), BF16), wide],
            2 * one,
        )

    bases, direct, (weights, within) = scan(sums, every, False, within_work, (qg_own, qg_other, kv_own, kv_other))
    att_own, att_send, d_attn, states, grad_every, *grad_sums = call(
        functools.partial(forward_kernel, share),
        "forward",
        [qg_own, qg_other, within, *bases, every, direct],
        [flat, flat, flat_two, every_shape, every_shape] + sums_shape,
        2 * one,
    )

    def middle_work(*operands):
        return call(functools.partial(middle_kernel, heads), "middle", operands, [flat, flat, wide, wide], 5 * one)

    bases, direct, (dq_own, dq_send, key_part, value_part) = scan(
        grad_sums, grad_every, True, middle_work, (qg_own, qg_other, kv_own, kv_other, d_attn, weights, states)
    )
    att_other, dq_other = swap(att_send, pair), swap(dq_send, pair)
    attended, grad_queries = call(
        join_kernel, "join", [att_own, att_other, dq_own, dq_other], [full] * 2, hbm_out=True, scratch=sems
    )
    dk_own, dv_own, dk_send, dv_send = call(
        functools.partial(final_kernel, share),
        "final",
        [kv_own, kv_other, key_part, value_part, *bases, grad_every, direct],
        [flat] * 4,
        2 * one,
    )
    dk_other, dv_other = swap(dk_send, pair), swap(dv_send, pair)
    grad_keys, grad_values = call(
        join_kernel, "join", [dk_own, dk_other, dv_own, dv_other], [full] * 2, hbm_out=True, scratch=sems
    )
    return (attended, grad_queries, grad_keys, grad_values)


def solution(mesh):
    spec = P(AXES, None)
    return jax.shard_map(body, mesh=mesh, in_specs=(spec,) * 4, out_specs=(spec,) * 4, check_vma=False)
```

```python
import functools

import jax
import jax.numpy as jnp
from jax import lax
from jax.experimental import pallas as pl
from jax.experimental.pallas import tpu as pltpu
from jax.sharding import PartitionSpec as P


DH = 128
AXES = ("context", "tensor")
PLANE = 8
GROUP = 4
OWNERS = 4

eps = 1e-06

F32 = jnp.float32
BF16 = jnp.bfloat16


def dot(a, b, contract):
    return lax.dot_general(a, b, ((contract[:1], contract[1:]), ((), ())), preferred_element_type=F32)


def pair_bit():
    pair = lax.axis_size(AXES[1]) if lax.axis_size(AXES[1]) < GROUP else 1
    return pair, (GROUP - 1) ^ pair, GROUP


def here():
    return lax.axis_index(AXES[0]) * lax.axis_size(AXES[1]) + lax.axis_index(AXES[1])


def has(bit):
    return jnp.bitwise_and(here(), bit) > 0


def owner_xor(r):
    _, near, far = pair_bit()
    return (near if r & 1 else 0) ^ (far if r & 2 else 0)


def owner():
    _, near, far = pair_bit()
    return has(near).astype(jnp.int32) + 2 * has(far).astype(jnp.int32)


def swap(x, bits):
    count = lax.axis_size(AXES[0]) * lax.axis_size(AXES[1])
    return lax.ppermute(x, AXES, [(i, i ^ bits) for i in range(count)])


def call(kernel, inputs, outs, flops=0, hbm_in=False, hbm_out=False, scratch=(), grant=16):
    space_in = pl.BlockSpec(memory_space=pl.ANY if hbm_in else pltpu.VMEM)
    space_out = pl.BlockSpec(memory_space=pl.ANY if hbm_out else pltpu.VMEM)
    moved = sum(a.size * a.dtype.itemsize for a in list(inputs) + list(outs))
    return pl.pallas_call(
        kernel,
        out_shape=list(outs),
        in_specs=[space_in] * len(inputs),
        out_specs=[space_out] * len(outs),
        scratch_shapes=list(scratch),
        compiler_params=pltpu.CompilerParams(vmem_limit_bytes=grant * 1024 * 1024),
        cost_estimate=pl.CostEstimate(flops=flops, bytes_accessed=moved, transcendentals=0),
    )(*inputs)


def share_columns(r, j, share):
    head = jnp.bitwise_xor(owner(), r) * share + j
    return head, pl.ds(pl.multiple_of(head * DH, DH), DH)


def causal_mask(rows):
    return lax.broadcasted_iota(jnp.int32, (rows, rows), 0) >= lax.broadcasted_iota(jnp.int32, (rows, rows), 1)


def run_copies(copies):
    for copy in copies:
        copy.start()
    for copy in copies:
        copy.wait()


def split_kernel(a, b, own, other, sems):
    half = own.shape[2]
    mine = has(pair_bit()[0]).astype(jnp.int32)
    copies = []
    for k, target in enumerate((other, own)):
        for n, source in enumerate((a, b)):
            at = pl.ds(pl.multiple_of((mine if k else 1 - mine) * half, half), half)
            copies.append(pltpu.make_async_copy(source.at[:, at], target.at[n], sems.at[n, k]))
    run_copies(copies)


def join_first_kernel(*refs):
    att_own, (dq_own, received), outs, sems = refs[:OWNERS], refs[OWNERS : OWNERS + 2], refs[OWNERS + 2 : -1], refs[-1]
    half, width = dq_own.shape[1], att_own[0].shape[1]
    mine = has(pair_bit()[0]).astype(jnp.int32)
    at = pl.ds(pl.multiple_of((1 - mine) * half, half), half)
    copies = [pltpu.make_async_copy(received.at[n], outs[n].at[:, at], sems.at[n]) for n in range(2)]
    at = pl.ds(pl.multiple_of(mine * half, half), half)
    copies.append(pltpu.make_async_copy(dq_own, outs[1].at[:, at], sems.at[2]))
    for r in range(OWNERS):
        at = pl.ds(pl.multiple_of(mine * half + jnp.bitwise_xor(owner(), r) * width, width), width)
        copies.append(pltpu.make_async_copy(att_own[r], outs[0].at[:, at], sems.at[3 + r]))
    run_copies(copies)


def join_last_kernel(*refs):
    own, received, outs, sems = refs[:OWNERS], refs[OWNERS : 2 * OWNERS], refs[2 * OWNERS : -1], refs[-1]
    width = own[0].shape[2]
    half = OWNERS * width
    mine = has(pair_bit()[0]).astype(jnp.int32)
    copies = []
    for r in range(OWNERS):
        for k, sources in enumerate((received, own)):
            start = (mine if k else 1 - mine) * half + jnp.bitwise_xor(owner(), r) * width
            for n in range(2):
                at = pl.ds(pl.multiple_of(start, width), width)
                copies.append(pltpu.make_async_copy(sources[r].at[n], outs[n].at[:, at], sems.at[r, k, n]))
    run_copies(copies)


def states_kernel(share, own, other, *outs):
    sums, every = outs[:OWNERS], outs[OWNERS]
    for r in range(OWNERS):
        for j in range(share):
            _, at = share_columns(r, j, share)
            first = dot(own[0, :, at], own[1, :, at], (0, 0))
            second = dot(other[0, :, at], other[1, :, at], (0, 0))
            every[r, 0, j] = first.astype(BF16)
            every[r, 1, j] = second.astype(BF16)
            sums[r][j] = (first + second).astype(BF16)


def sum_kernel(*refs):
    for j in range(refs[0].shape[0]):
        refs[-1][j] = sum(ref[j].astype(F32) for ref in refs[:-1]).astype(BF16)


def pack_kernel(*refs):
    for r in range(OWNERS):
        refs[-1][r] = refs[r][...]


def base_kernel(reverse, steps, *refs):
    count = len(steps)
    parts, others, (mine, across) = refs[:OWNERS], refs[OWNERS : OWNERS + count], refs[OWNERS + count :]
    late = has(pair_bit()[2])
    counts_far = jnp.logical_not(late) if reverse else late
    plane = here() // PLANE
    for j in range(mine.shape[0]):
        base = jnp.zeros(mine.shape[1:], F32)
        for other, step in zip(others, steps):
            source = jnp.bitwise_xor(plane, step)
            keep = source > plane if reverse else source < plane
            base = base + jnp.where(keep, other[j].astype(F32), 0.0)
        same = parts[0][j].astype(F32) + parts[1][j].astype(F32)
        far = parts[2][j].astype(F32) + parts[3][j].astype(F32)
        mine[j] = (base + jnp.where(counts_far, far, 0.0)).astype(BF16)
        across[j] = (base + jnp.where(counts_far, 0.0, same)).astype(BF16)


def local_kernel(reverse, every, direct, out):
    pair, near, _ = pair_bit()
    place = jnp.bitwise_and(here(), GROUP - 1)
    for r in range(OWNERS):
        for j in range(every.shape[2]):
            sources = [(0, every[r, 0, j]), (pair, every[r, 1, j])]
            sources += [(near, direct[r ^ 1, 0, j]), (near ^ pair, direct[r ^ 1, 1, j])]
            sources = [(mask, state.astype(F32)) for mask, state in sources]
            for n, target in enumerate((0, pair)):
                to = jnp.bitwise_xor(place, target)
                total = jnp.zeros(every.shape[3:], F32)
                for mask, state in sources:
                    if mask != target:
                        source = jnp.bitwise_xor(place, mask)
                        total = total + jnp.where(source > to if reverse else source < to, state, 0.0)
                out[r, n, j] = total


def within_kernel(heads, qg_own, qg_other, kv_own, kv_other, weights, attn):
    causal = causal_mask(qg_own.shape[1])
    for n, (qg, kv) in enumerate(((qg_own, kv_own), (qg_other, kv_other))):
        for h in range(heads):
            at = slice(h * DH, (h + 1) * DH)
            w = jnp.where(causal, dot(qg[0, :, at], kv[0, :, at], (1, 1)), 0.0).astype(BF16)
            weights[n, h] = w
            attn[n, :, at] = dot(w, kv[1, :, at], (1, 0))


def forward_kernel(share, r, qg_own, qg_other, within, base, local, grad_sum, att_own, att_other, d_attn, states, every):
    for j in range(share):
        _, at = share_columns(r, j, share)
        to = slice(j * DH, (j + 1) * DH)
        before = base[j].astype(F32)
        total = 0.0
        for n, (qg, out) in enumerate(((qg_own, att_own), (qg_other, att_other))):
            state = (before + local[r, n, j]).astype(BF16)
            states[n, j] = state
            query = qg[0, :, at]
            attn = within[n, :, at] + dot(query, state, (1, 0))
            inverse = 1.0 / jnp.sqrt(jnp.mean(attn * attn, axis=1, keepdims=True) + eps)
            normed = attn * inverse
            out[:, to] = normed.astype(BF16)
            cotangent = qg[1, :, at].astype(F32)
            inner = jnp.mean(cotangent * normed, axis=1, keepdims=True)
            d = ((cotangent - normed * inner) * inverse).astype(BF16)
            d_attn[n, :, to] = d
            grad = dot(query, d, (0, 0))
            every[n, j] = grad.astype(BF16)
            total = total + grad
        grad_sum[j] = total.astype(BF16)


def middle_kernel(share, qg_own, qg_other, kv_own, kv_other, weights, *refs):
    d_attn, states, att_other = refs[:OWNERS], refs[OWNERS : 2 * OWNERS], refs[2 * OWNERS : 3 * OWNERS]
    dq_own, send, key_part, value_part = refs[3 * OWNERS :]
    causal = causal_mask(qg_own.shape[1])
    for r in range(OWNERS):
        for j in range(share):
            head, at = share_columns(r, j, share)
            to = slice(j * DH, (j + 1) * DH)
            send[0, :, at] = att_other[r][:, to]
            for n, (qg, kv) in enumerate(((qg_own, kv_own), (qg_other, kv_other))):
                d = d_attn[r][n, :, to]
                dw = jnp.where(causal, dot(d, kv[1, :, at], (1, 1)), 0.0).astype(BF16)
                d_query = (dot(dw, kv[0, :, at], (1, 0)) + dot(d, states[r][n, j], (1, 1))).astype(BF16)
                if n == 0:
                    dq_own[:, at] = d_query
                else:
                    send[1, :, at] = d_query
                key_part[n, :, at] = dot(dw, qg[0, :, at], (0, 0))
                value_part[n, :, at] = dot(weights[n, head], d, (0, 0))


def final_kernel(share, r, kv_own, kv_other, key_part, value_part, base, local, own, send):
    for j in range(share):
        _, at = share_columns(r, j, share)
        to = slice(j * DH, (j + 1) * DH)
        after = base[j].astype(F32)
        for n, (kv, out) in enumerate(((kv_own, own), (kv_other, send))):
            state = (after + local[r, n, j]).astype(BF16)
            out[0, :, to] = (key_part[n, :, at] + dot(kv[1, :, at], state, (1, 1))).astype(BF16)
            out[1, :, to] = (value_part[n, :, at] + dot(kv[0, :, at], state, (1, 0))).astype(BF16)


def radices(planes):
    bits, found = 1, []
    while bits < planes:
        masks = [bits, 2 * bits, 3 * bits] if 2 * bits < planes else [bits]
        found.append(masks)
        bits *= 4
    return found


def scan(sums, every, reverse, work, later):
    count = lax.axis_size(AXES[0]) * lax.axis_size(AXES[1])
    _, near, _ = pair_bit()
    received = [sums[0]] + [None] * (OWNERS - 1)
    for r in (3, 2, 1):
        received[r] = swap(sums[r], owner_xor(r))
    direct = swap(every, near)
    shape = jax.ShapeDtypeStruct(sums[0].shape, BF16)
    (total,) = call(sum_kernel, received, [shape], grant=4)
    total, later = lax.optimization_barrier((total, later))
    others, steps = [], []
    levels = radices(count // PLANE)
    for level, masks in enumerate(levels):
        got = [swap(total, mask * PLANE) for mask in reversed(masks)]
        others, steps = others + got, steps + masks[::-1]
        if level + 1 < len(levels):
            (total,) = call(sum_kernel, [total, *got], [shape], grant=4)
    done = work(*later)
    others, done = lax.optimization_barrier((others, done))
    mine, across = call(functools.partial(base_kernel, reverse, steps), [*received, *others], [shape] * 2, grant=4)
    (local,) = call(functools.partial(local_kernel, reverse), [every, direct], [jax.ShapeDtypeStruct(every.shape, F32)])
    bases = [mine] + [None] * (OWNERS - 1)
    for r in (3, 2, 1):
        bases[r] = swap(across if r & 2 else mine, owner_xor(r))
    return bases, local, done


def body(queries, key_rows, value_rows, grad_output):
    rows, width = queries.shape
    half = width // 2
    heads = half // DH
    share = heads // OWNERS
    count = lax.axis_size(AXES[0]) * lax.axis_size(AXES[1])
    assert count % PLANE == 0 and count & (count - 1) == 0 and heads % OWNERS == 0
    pair = pair_bit()[0]
    one = 4 * rows * half * DH
    of = jax.ShapeDtypeStruct
    flat, flat_two, wide = of((rows, half), BF16), of((2, rows, half), BF16), of((2, rows, half), F32)
    full = of((rows, width), BF16)
    part, part_two = of((rows, share * DH), BF16), of((2, rows, share * DH), BF16)
    state, state_two = of((share, DH, DH), BF16), of((2, share, DH, DH), BF16)
    state_all = of((OWNERS, 2, share, DH, DH), BF16)
    sems = pltpu.SemaphoreType.DMA

    kv_own, kv_send = call(
        split_kernel, [key_rows, value_rows], [flat_two] * 2, hbm_in=True, scratch=[sems((2, 2))], grant=53
    )
    kv_other = swap(kv_send, pair)
    *sums, every = call(
        functools.partial(states_kernel, share), [kv_own, kv_other], [state] * OWNERS + [state_all], one
    )
    queries, grad_output, *sums = lax.optimization_barrier((queries, grad_output, *sums))
    qg_own, qg_send = call(split_kernel, [queries, grad_output], [flat_two] * 2, hbm_in=True, scratch=[sems((2, 2))])
    qg_other = swap(qg_send, pair)

    def within_work(*operands):
        return call(
            functools.partial(within_kernel, heads), operands, [of((2, heads, rows, rows), BF16), wide], 2 * one
        )

    bases, local, (weights, within) = scan(sums, every, False, within_work, (qg_own, qg_other, kv_own, kv_other))
    results = [None] * OWNERS
    for r in (0, 3, 2, 1):
        results[r] = call(
            functools.partial(forward_kernel, share, r),
            [qg_own, qg_other, within, bases[r], local],
            [state, part, part, part_two, state_two, state_two],
            2 * one // OWNERS,
        )
    grad_sums, att_own, att_other, d_attn, states, grad_every = zip(*results)
    (every,) = call(pack_kernel, grad_every, [state_all])

    def middle_work(*operands):
        return call(functools.partial(middle_kernel, share), operands, [flat, flat_two, wide, wide], 5 * one)

    bases, local, (dq_own, send, key_part, value_part) = scan(
        grad_sums, every, True, middle_work, (qg_own, qg_other, kv_own, kv_other, weights, *d_attn, *states, *att_other)
    )
    attended, grad_queries = call(
        join_first_kernel, [*att_own, dq_own, swap(send, pair)], [full] * 2, hbm_out=True, scratch=[sems((3 + OWNERS,))]
    )
    bases[1], attended, grad_queries = lax.optimization_barrier((bases[1], attended, grad_queries))
    own, received = [None] * OWNERS, [None] * OWNERS
    for r in (0, 3, 2, 1):
        own[r], send = call(
            functools.partial(final_kernel, share, r),
            [kv_own, kv_other, key_part, value_part, bases[r], local],
            [part_two] * 2,
            2 * one // OWNERS,
        )
        received[r] = swap(send, pair)
    grad_keys, grad_values = call(
        join_last_kernel, [*own, *received], [full] * 2, hbm_out=True, scratch=[sems((OWNERS, 2, 2))]
    )
    return (attended, grad_queries, grad_keys, grad_values)


def solution(mesh):
    spec = P(AXES, None)

    return jax.shard_map(body, mesh=mesh, in_specs=(spec,) * 4, out_specs=(spec,) * 4, check_vma=False)
```

```python
import functools

import jax
import jax.numpy as jnp
from jax import lax
from jax.experimental import pallas as pl
from jax.experimental.pallas import tpu as pltpu
from jax.sharding import PartitionSpec as P


DH = 128
AXES = ("context", "tensor")
PLANE = 8
GROUP = 4
OWNERS = 4
ARRIVAL = (0, 3, 2, 1)

eps = 1e-06

F32 = jnp.float32
BF16 = jnp.bfloat16


def dot(a, b, contract):
    return lax.dot_general(a, b, ((contract[:1], contract[1:]), ((), ())), preferred_element_type=F32)


def pair_bit():
    pair = lax.axis_size(AXES[1]) if lax.axis_size(AXES[1]) < GROUP else 1
    return pair, (GROUP - 1) ^ pair, GROUP


def here():
    return lax.axis_index(AXES[0]) * lax.axis_size(AXES[1]) + lax.axis_index(AXES[1])


def has(bit):
    return jnp.bitwise_and(here(), bit) > 0


def owner_xor(r):
    _, near, far = pair_bit()
    return (near if r & 1 else 0) ^ (far if r & 2 else 0)


def owner():
    _, near, far = pair_bit()
    return has(near).astype(jnp.int32) + 2 * has(far).astype(jnp.int32)


def swap(x, bits):
    count = lax.axis_size(AXES[0]) * lax.axis_size(AXES[1])
    return lax.ppermute(x, AXES, [(i, i ^ bits) for i in range(count)])


def call(kernel, inputs, outs, flops=0, hbm_in=False, hbm_out=False, scratch=(), grant=16, alias=0):
    space_in = pl.BlockSpec(memory_space=pl.ANY if hbm_in else pltpu.VMEM)
    space_out = pl.BlockSpec(memory_space=pl.ANY if hbm_out else pltpu.VMEM)
    moved = sum(a.size * a.dtype.itemsize for a in list(inputs) + list(outs))
    return pl.pallas_call(
        kernel,
        out_shape=list(outs),
        in_specs=[pl.BlockSpec(memory_space=pl.ANY)] * alias + [space_in] * (len(inputs) - alias),
        out_specs=[space_out] * len(outs),
        scratch_shapes=list(scratch),
        input_output_aliases={n: n for n in range(alias)},
        compiler_params=pltpu.CompilerParams(vmem_limit_bytes=grant * 1024 * 1024),
        cost_estimate=pl.CostEstimate(flops=flops, bytes_accessed=moved, transcendentals=0),
    )(*inputs)


def share_columns(r, j, share):
    head = jnp.bitwise_xor(owner(), r) * share + j
    return head, pl.ds(pl.multiple_of(head * DH, DH), DH)


def causal_mask(rows):
    return lax.broadcasted_iota(jnp.int32, (rows, rows), 0) >= lax.broadcasted_iota(jnp.int32, (rows, rows), 1)


def run_copies(copies):
    for copy in copies:
        copy.start()
    for copy in copies:
        copy.wait()


def half_columns(partner):
    mine = has(pair_bit()[0]).astype(jnp.int32)
    return 1 - mine if partner else mine


def split_kernel(partner, a, b, out, sems):
    _, rows, half = out.shape
    chunks = sems.shape[1]
    at = pl.ds(pl.multiple_of(half_columns(partner) * half, half), half)
    copies = []
    for k in range(chunks):
        take = slice(k * rows // chunks, (k + 1) * rows // chunks)
        for n, source in enumerate((a, b)):
            copies.append(pltpu.make_async_copy(source.at[take, at], out.at[n, take], sems.at[n, k]))
    run_copies(copies)


def write_half(source, target, partner, sem):
    half = source.shape[1]
    at = pl.ds(pl.multiple_of(half_columns(partner) * half, half), half)
    return pltpu.make_async_copy(source, target.at[:, at], sem)


def write_share(source, target, partner, r, sem):
    width = source.shape[1]
    start = (half_columns(partner) * OWNERS + jnp.bitwise_xor(owner(), r)) * width
    return pltpu.make_async_copy(source, target.at[:, pl.ds(pl.multiple_of(start, width), width)], sem)


def join_own_kernel(*refs):
    att_own, dq_own, (attended, grad_queries), sems = refs[:OWNERS], refs[OWNERS], refs[OWNERS + 1 : -1], refs[-1]
    copies = [write_half(dq_own, grad_queries, False, sems.at[OWNERS])]
    copies += [write_share(att_own[r], attended, False, r, sems.at[r]) for r in range(OWNERS)]
    run_copies(copies)


def join_most_kernel(count, *refs):
    swapped, own = refs[2], refs[3 : 3 + OWNERS]
    received, outs, sems = refs[3 + OWNERS : 3 + OWNERS + count], refs[3 + OWNERS + count : -1], refs[-1]
    copies = []
    for n in range(2):
        copies.append(write_half(swapped.at[n], outs[n], True, sems.at[0, n]))
        for r in range(OWNERS):
            copies.append(write_share(own[r].at[n], outs[2 + n], False, r, sems.at[1 + r, n]))
        for k, r in enumerate(ARRIVAL[:count]):
            copies.append(write_share(received[k].at[n], outs[2 + n], True, r, sems.at[1 + OWNERS + k, n]))
    run_copies(copies)


def join_rest_kernel(count, *refs):
    received, outs, sems = refs[2 : 2 + OWNERS - count], refs[2 + OWNERS - count : -1], refs[-1]
    copies = []
    for k, r in enumerate(ARRIVAL[count:]):
        copies += [write_share(received[k].at[n], outs[n], True, r, sems.at[k, n]) for n in range(2)]
    run_copies(copies)


def states_kernel(share, own, other, *outs):
    sums, every = outs[:OWNERS], outs[OWNERS]
    for r in range(OWNERS):
        for j in range(share):
            _, at = share_columns(r, j, share)
            first = dot(own[0, :, at], own[1, :, at], (0, 0))
            second = dot(other[0, :, at], other[1, :, at], (0, 0))
            every[r, 0, j] = first.astype(BF16)
            every[r, 1, j] = second.astype(BF16)
            sums[r][j] = (first + second).astype(BF16)


def sum_kernel(*refs):
    for j in range(refs[0].shape[0]):
        refs[-1][j] = sum(ref[j].astype(F32) for ref in refs[:-1]).astype(BF16)


def pack_kernel(*refs):
    for r in range(OWNERS):
        refs[-1][r] = refs[r][...]


def base_kernel(reverse, steps, *refs):
    count = len(steps)
    parts, others, (mine, across) = refs[:OWNERS], refs[OWNERS : OWNERS + count], refs[OWNERS + count :]
    late = has(pair_bit()[2])
    counts_far = jnp.logical_not(late) if reverse else late
    plane = here() // PLANE
    for j in range(mine.shape[0]):
        base = jnp.zeros(mine.shape[1:], F32)
        for other, step in zip(others, steps):
            source = jnp.bitwise_xor(plane, step)
            keep = source > plane if reverse else source < plane
            base = base + jnp.where(keep, other[j].astype(F32), 0.0)
        same = parts[0][j].astype(F32) + parts[1][j].astype(F32)
        far = parts[2][j].astype(F32) + parts[3][j].astype(F32)
        mine[j] = (base + jnp.where(counts_far, far, 0.0)).astype(BF16)
        across[j] = (base + jnp.where(counts_far, 0.0, same)).astype(BF16)


def local_kernel(reverse, every, direct, out):
    pair, near, _ = pair_bit()
    place = jnp.bitwise_and(here(), GROUP - 1)
    for r in range(OWNERS):
        for j in range(every.shape[2]):
            sources = [(0, every[r, 0, j]), (pair, every[r, 1, j])]
            sources += [(near, direct[r ^ 1, 0, j]), (near ^ pair, direct[r ^ 1, 1, j])]
            sources = [(mask, state.astype(F32)) for mask, state in sources]
            for n, target in enumerate((0, pair)):
                to = jnp.bitwise_xor(place, target)
                total = jnp.zeros(every.shape[3:], F32)
                for mask, state in sources:
                    if mask != target:
                        source = jnp.bitwise_xor(place, mask)
                        total = total + jnp.where(source > to if reverse else source < to, state, 0.0)
                out[r, n, j] = total


def within_kernel(heads, qg_own, qg_other, kv_own, kv_other, weights, attn):
    causal = causal_mask(qg_own.shape[1])
    for n, (qg, kv) in enumerate(((qg_own, kv_own), (qg_other, kv_other))):
        for h in range(heads):
            at = slice(h * DH, (h + 1) * DH)
            w = jnp.where(causal, dot(qg[0, :, at], kv[0, :, at], (1, 1)), 0.0).astype(BF16)
            weights[n, h] = w
            attn[n, :, at] = dot(w, kv[1, :, at], (1, 0))


def forward_kernel(share, r, qg_own, qg_other, within, base, local, grad_sum, att_own, att_other, d_attn, states, every):
    for j in range(share):
        _, at = share_columns(r, j, share)
        to = slice(j * DH, (j + 1) * DH)
        before = base[j].astype(F32)
        total = 0.0
        for n, (qg, out) in enumerate(((qg_own, att_own), (qg_other, att_other))):
            state = (before + local[r, n, j]).astype(BF16)
            states[n, j] = state
            query = qg[0, :, at]
            attn = within[n, :, at] + dot(query, state, (1, 0))
            inverse = 1.0 / jnp.sqrt(jnp.mean(attn * attn, axis=1, keepdims=True) + eps)
            normed = attn * inverse
            out[:, to] = normed.astype(BF16)
            cotangent = qg[1, :, at].astype(F32)
            inner = jnp.mean(cotangent * normed, axis=1, keepdims=True)
            d = ((cotangent - normed * inner) * inverse).astype(BF16)
            d_attn[n, :, to] = d
            grad = dot(query, d, (0, 0))
            every[n, j] = grad.astype(BF16)
            total = total + grad
        grad_sum[j] = total.astype(BF16)


def middle_kernel(share, qg_own, qg_other, kv_own, kv_other, weights, *refs):
    d_attn, states, att_other = refs[:OWNERS], refs[OWNERS : 2 * OWNERS], refs[2 * OWNERS : 3 * OWNERS]
    dq_own, send, key_part, value_part = refs[3 * OWNERS :]
    causal = causal_mask(qg_own.shape[1])
    for r in range(OWNERS):
        for j in range(share):
            head, at = share_columns(r, j, share)
            to = slice(j * DH, (j + 1) * DH)
            send[0, :, at] = att_other[r][:, to]
            for n, (qg, kv) in enumerate(((qg_own, kv_own), (qg_other, kv_other))):
                d = d_attn[r][n, :, to]
                dw = jnp.where(causal, dot(d, kv[1, :, at], (1, 1)), 0.0).astype(BF16)
                d_query = (dot(dw, kv[0, :, at], (1, 0)) + dot(d, states[r][n, j], (1, 1))).astype(BF16)
                if n == 0:
                    dq_own[:, at] = d_query
                else:
                    send[1, :, at] = d_query
                key_part[n, :, at] = dot(dw, qg[0, :, at], (0, 0))
                value_part[n, :, at] = dot(weights[n, head], d, (0, 0))


def final_kernel(share, r, kv_own, kv_other, key_part, value_part, base, local, own, send):
    for j in range(share):
        _, at = share_columns(r, j, share)
        to = slice(j * DH, (j + 1) * DH)
        after = base[j].astype(F32)
        for n, (kv, out) in enumerate(((kv_own, own), (kv_other, send))):
            state = (after + local[r, n, j]).astype(BF16)
            out[0, :, to] = (key_part[n, :, at] + dot(kv[1, :, at], state, (1, 1))).astype(BF16)
            out[1, :, to] = (value_part[n, :, at] + dot(kv[0, :, at], state, (1, 0))).astype(BF16)


def radices(planes):
    bits, found = 1, []
    while bits < planes:
        masks = [bits, 2 * bits, 3 * bits] if 2 * bits < planes else [bits]
        found.append(masks)
        bits *= 4
    return found


def scan(sums, every, reverse, work, later):
    count = lax.axis_size(AXES[0]) * lax.axis_size(AXES[1])
    _, near, _ = pair_bit()
    received = [sums[0]] + [None] * (OWNERS - 1)
    for r in (3, 2, 1):
        received[r] = swap(sums[r], owner_xor(r))
    direct = swap(every, near)
    shape = jax.ShapeDtypeStruct(sums[0].shape, BF16)
    (total,) = call(sum_kernel, received, [shape], grant=4)
    total, later = lax.optimization_barrier((total, later))
    others, steps = [], []
    levels = radices(count // PLANE)
    for level, masks in enumerate(levels):
        got = [swap(total, mask * PLANE) for mask in reversed(masks)]
        others, steps = others + got, steps + masks[::-1]
        if level + 1 < len(levels):
            (total,) = call(sum_kernel, [total, *got], [shape], grant=4)
    done = work(*later)
    others, done = lax.optimization_barrier((others, done))
    mine, across = call(functools.partial(base_kernel, reverse, steps), [*received, *others], [shape] * 2, grant=4)
    (local,) = call(functools.partial(local_kernel, reverse), [every, direct], [jax.ShapeDtypeStruct(every.shape, F32)])
    bases = [mine] + [None] * (OWNERS - 1)
    for r in (3, 2, 1):
        bases[r] = swap(across if r & 2 else mine, owner_xor(r))
    return bases, local, done


def body(queries, key_rows, value_rows, grad_output):
    rows, width = queries.shape
    half = width // 2
    heads = half // DH
    share = heads // OWNERS
    count = lax.axis_size(AXES[0]) * lax.axis_size(AXES[1])
    assert count % PLANE == 0 and count & (count - 1) == 0 and heads % OWNERS == 0
    pair = pair_bit()[0]
    one = 4 * rows * half * DH
    of = jax.ShapeDtypeStruct
    flat, flat_two, wide = of((rows, half), BF16), of((2, rows, half), BF16), of((2, rows, half), F32)
    full = of((rows, width), BF16)
    part, part_two = of((rows, share * DH), BF16), of((2, rows, share * DH), BF16)
    state, state_two = of((share, DH, DH), BF16), of((2, share, DH, DH), BF16)
    state_all = of((OWNERS, 2, share, DH, DH), BF16)
    sems = pltpu.SemaphoreType.DMA

    kv_send, kv_own = (
        call(
            functools.partial(split_kernel, partner),
            [key_rows, value_rows],
            [flat_two],
            hbm_in=True,
            scratch=[sems((2, 4))],
            grant=53,
        )[0]
        for partner in (True, False)
    )
    kv_other = swap(kv_send, pair)
    *sums, every = call(
        functools.partial(states_kernel, share), [kv_own, kv_other], [state] * OWNERS + [state_all], one
    )
    queries, grad_output, *sums = lax.optimization_barrier((queries, grad_output, *sums))
    qg_send, qg_own = (
        call(
            functools.partial(split_kernel, partner),
            [queries, grad_output],
            [flat_two],
            hbm_in=True,
            scratch=[sems((2, 1))],
        )[0]
        for partner in (True, False)
    )
    qg_other = swap(qg_send, pair)

    def within_work(*operands):
        return call(
            functools.partial(within_kernel, heads), operands, [of((2, heads, rows, rows), BF16), wide], 2 * one
        )

    bases, local, (weights, within) = scan(sums, every, False, within_work, (qg_own, qg_other, kv_own, kv_other))
    results = [None] * OWNERS
    for r in ARRIVAL:
        results[r] = call(
            functools.partial(forward_kernel, share, r),
            [qg_own, qg_other, within, bases[r], local],
            [state, part, part, part_two, state_two, state_two],
            2 * one // OWNERS,
        )
    grad_sums, att_own, att_other, d_attn, states, grad_every = zip(*results)
    (every,) = call(pack_kernel, grad_every, [state_all])

    def middle_work(*operands):
        return call(functools.partial(middle_kernel, share), operands, [flat, flat_two, wide, wide], 5 * one)

    bases, local, (dq_own, send, key_part, value_part) = scan(
        grad_sums, every, True, middle_work, (qg_own, qg_other, kv_own, kv_other, weights, *d_attn, *states, *att_other)
    )
    swapped = swap(send, pair)
    attended, grad_queries = call(
        join_own_kernel, [*att_own, dq_own], [full] * 2, hbm_out=True, scratch=[sems((OWNERS + 1,))]
    )
    own, received = [None] * OWNERS, [None] * OWNERS
    for r in ARRIVAL:
        own[r], send = call(
            functools.partial(final_kernel, share, r),
            [kv_own, kv_other, key_part, value_part, bases[r], local],
            [part_two] * 2,
            2 * one // OWNERS,
        )
        received[r] = swap(send, pair)
    early = OWNERS - 1
    attended, grad_queries, grad_keys, grad_values = call(
        functools.partial(join_most_kernel, early),
        [attended, grad_queries, swapped, *own, *(received[r] for r in ARRIVAL[:early])],
        [full] * 4,
        hbm_out=True,
        scratch=[sems((1 + OWNERS + early, 2))],
        alias=2,
    )
    grad_keys, grad_values = call(
        functools.partial(join_rest_kernel, early),
        [grad_keys, grad_values, *(received[r] for r in ARRIVAL[early:])],
        [full] * 2,
        hbm_out=True,
        scratch=[sems((OWNERS - early, 2))],
        alias=2,
    )
    return (attended, grad_queries, grad_keys, grad_values)


def solution(mesh):
    spec = P(AXES, None)

    return jax.shard_map(body, mesh=mesh, in_specs=(spec,) * 4, out_specs=(spec,) * 4, check_vma=False)
```

```python
import functools

import jax
import jax.numpy as jnp
from jax import lax
from jax.experimental import pallas as pl
from jax.experimental.pallas import tpu as pltpu
from jax.sharding import PartitionSpec as P


DH = 128
AXES = ("context", "tensor")
PLANE = 8
GROUP = 4
OWNERS = 4
OUT = (3, 1, 2)
BACK = (0, 3, 1, 2)
ARRIVAL = (0, 3, 1, 2)

eps = 1e-06

F32 = jnp.float32
BF16 = jnp.bfloat16


def dot(a, b, contract):
    return lax.dot_general(a, b, ((contract[:1], contract[1:]), ((), ())), preferred_element_type=F32)


def pair_bit():
    pair = lax.axis_size(AXES[1]) if lax.axis_size(AXES[1]) < GROUP else 1
    return pair, (GROUP - 1) ^ pair, GROUP


def here():
    return lax.axis_index(AXES[0]) * lax.axis_size(AXES[1]) + lax.axis_index(AXES[1])


def has(bit):
    return jnp.bitwise_and(here(), bit) > 0


def owner_xor(r):
    _, near, far = pair_bit()
    return (near if r & 1 else 0) ^ (far if r & 2 else 0)


def owner():
    _, near, far = pair_bit()
    return has(near).astype(jnp.int32) + 2 * has(far).astype(jnp.int32)


def swap(x, bits):
    count = lax.axis_size(AXES[0]) * lax.axis_size(AXES[1])
    return lax.ppermute(x, AXES, [(i, i ^ bits) for i in range(count)])


def call(kernel, inputs, outs, flops=0, hbm_in=False, hbm_out=False, scratch=(), grant=16, alias=0):
    space_in = pl.BlockSpec(memory_space=pl.ANY if hbm_in else pltpu.VMEM)
    space_out = pl.BlockSpec(memory_space=pl.ANY if hbm_out else pltpu.VMEM)
    moved = sum(a.size * a.dtype.itemsize for a in list(inputs) + list(outs))
    return pl.pallas_call(
        kernel,
        out_shape=list(outs),
        in_specs=[pl.BlockSpec(memory_space=pl.ANY)] * alias + [space_in] * (len(inputs) - alias),
        out_specs=[space_out] * len(outs),
        scratch_shapes=list(scratch),
        input_output_aliases={n: n for n in range(alias)},
        compiler_params=pltpu.CompilerParams(vmem_limit_bytes=grant * 1024 * 1024),
        cost_estimate=pl.CostEstimate(flops=flops, bytes_accessed=moved, transcendentals=0),
    )(*inputs)


def share_columns(r, j, share):
    head = jnp.bitwise_xor(owner(), r) * share + j
    return head, pl.ds(pl.multiple_of(head * DH, DH), DH)


def causal_mask(rows):
    return lax.broadcasted_iota(jnp.int32, (rows, rows), 0) >= lax.broadcasted_iota(jnp.int32, (rows, rows), 1)


def run_copies(copies):
    for copy in copies:
        copy.start()
    for copy in copies:
        copy.wait()


def half_columns(partner):
    mine = has(pair_bit()[0]).astype(jnp.int32)
    return 1 - mine if partner else mine


def split_kernel(partner, a, b, out, sems):
    _, rows, half = out.shape
    chunks = sems.shape[1]
    at = pl.ds(pl.multiple_of(half_columns(partner) * half, half), half)
    copies = []
    for k in range(chunks):
        take = slice(k * rows // chunks, (k + 1) * rows // chunks)
        for n, source in enumerate((a, b)):
            copies.append(pltpu.make_async_copy(source.at[take, at], out.at[n, take], sems.at[n, k]))
    run_copies(copies)


def write_half(source, target, partner, sem):
    half = source.shape[1]
    at = pl.ds(pl.multiple_of(half_columns(partner) * half, half), half)
    return pltpu.make_async_copy(source, target.at[:, at], sem)


def write_share(source, target, partner, r, sem):
    width = source.shape[1]
    start = (half_columns(partner) * OWNERS + jnp.bitwise_xor(owner(), r)) * width
    return pltpu.make_async_copy(source, target.at[:, pl.ds(pl.multiple_of(start, width), width)], sem)


def join_own_kernel(*refs):
    att_own, dq_own, (attended, grad_queries), sems = refs[:OWNERS], refs[OWNERS], refs[OWNERS + 1 : -1], refs[-1]
    copies = [write_half(dq_own, grad_queries, False, sems.at[OWNERS])]
    copies += [write_share(att_own[r], attended, False, r, sems.at[r]) for r in range(OWNERS)]
    run_copies(copies)


def join_most_kernel(count, *refs):
    swapped, own = refs[2], refs[3 : 3 + OWNERS]
    received, outs, sems = refs[3 + OWNERS : 3 + OWNERS + count], refs[3 + OWNERS + count : -1], refs[-1]
    copies = []
    for n in range(2):
        copies.append(write_half(swapped.at[n], outs[n], True, sems.at[0, n]))
        for r in range(OWNERS):
            copies.append(write_share(own[r].at[n], outs[2 + n], False, r, sems.at[1 + r, n]))
        for k, r in enumerate(ARRIVAL[:count]):
            copies.append(write_share(received[k].at[n], outs[2 + n], True, r, sems.at[1 + OWNERS + k, n]))
    run_copies(copies)


def join_rest_kernel(count, *refs):
    received, outs, sems = refs[2 : 2 + OWNERS - count], refs[2 + OWNERS - count : -1], refs[-1]
    copies = []
    for k, r in enumerate(ARRIVAL[count:]):
        copies += [write_share(received[k].at[n], outs[n], True, r, sems.at[k, n]) for n in range(2)]
    run_copies(copies)


def states_kernel(share, own, other, *outs):
    sums, every = outs[:OWNERS], outs[OWNERS]
    for r in range(OWNERS):
        for j in range(share):
            _, at = share_columns(r, j, share)
            first = dot(own[0, :, at], own[1, :, at], (0, 0))
            second = dot(other[0, :, at], other[1, :, at], (0, 0))
            every[r, 0, j] = first.astype(BF16)
            every[r, 1, j] = second.astype(BF16)
            sums[r][j] = (first + second).astype(BF16)


def sum_kernel(*refs):
    for j in range(refs[0].shape[0]):
        refs[-1][j] = sum(ref[j].astype(F32) for ref in refs[:-1]).astype(BF16)


def pack_kernel(*refs):
    for r in range(OWNERS):
        refs[-1][r] = refs[r][...]


def base_kernel(reverse, steps, *refs):
    count = len(steps)
    parts, others, (mine, across) = refs[:OWNERS], refs[OWNERS : OWNERS + count], refs[OWNERS + count :]
    late = has(pair_bit()[2])
    counts_far = jnp.logical_not(late) if reverse else late
    plane = here() // PLANE
    for j in range(mine.shape[0]):
        base = jnp.zeros(mine.shape[1:], F32)
        for other, step in zip(others, steps):
            source = jnp.bitwise_xor(plane, step)
            keep = source > plane if reverse else source < plane
            base = base + jnp.where(keep, other[j].astype(F32), 0.0)
        same = parts[0][j].astype(F32) + parts[1][j].astype(F32)
        far = parts[2][j].astype(F32) + parts[3][j].astype(F32)
        mine[j] = (base + jnp.where(counts_far, far, 0.0)).astype(BF16)
        across[j] = (base + jnp.where(counts_far, 0.0, same)).astype(BF16)


def local_kernel(reverse, every, direct, out):
    pair, near, _ = pair_bit()
    place = jnp.bitwise_and(here(), GROUP - 1)
    for r in range(OWNERS):
        for j in range(every.shape[2]):
            sources = [(0, every[r, 0, j]), (pair, every[r, 1, j])]
            sources += [(near, direct[r ^ 1, 0, j]), (near ^ pair, direct[r ^ 1, 1, j])]
            sources = [(mask, state.astype(F32)) for mask, state in sources]
            for n, target in enumerate((0, pair)):
                to = jnp.bitwise_xor(place, target)
                total = jnp.zeros(every.shape[3:], F32)
                for mask, state in sources:
                    if mask != target:
                        source = jnp.bitwise_xor(place, mask)
                        total = total + jnp.where(source > to if reverse else source < to, state, 0.0)
                out[r, n, j] = total


def within_kernel(heads, qg, kv, weights, attn):
    causal = causal_mask(qg.shape[1])
    for h in range(heads):
        at = slice(h * DH, (h + 1) * DH)
        w = jnp.where(causal, dot(qg[0, :, at], kv[0, :, at], (1, 1)), 0.0).astype(BF16)
        weights[h] = w
        attn[:, at] = dot(w, kv[1, :, at], (1, 0))


def forward_kernel(
    share, r, qg_own, qg_other, within_own, within_other, base, local, grad_sum, att_own, att_other, d_attn, states, every
):
    source, within, target = (qg_own, qg_other), (within_own, within_other), (att_own, att_other)

    def mean(x):
        return jnp.mean(x, axis=1, keepdims=True)

    for group in [[(j, n) for j in range(share) for n in range(2)]]:
        at = {j: share_columns(r, j, share)[1] for j, _ in group}
        to = {j: slice(j * DH, (j + 1) * DH) for j, _ in group}
        state = {(j, n): (base[j].astype(F32) + local[r, n, j]).astype(BF16) for j, n in group}
        query = {(j, n): source[n][0, :, at[j]] for j, n in group}
        attn = {(j, n): within[n][:, at[j]] + dot(query[j, n], state[j, n], (1, 0)) for j, n in group}
        inverse = {i: lax.rsqrt(mean(attn[i] * attn[i]) + eps) for i in group}
        normed = {i: attn[i] * inverse[i] for i in group}
        cotangent = {(j, n): source[n][1, :, at[j]].astype(F32) for j, n in group}
        inner = {i: mean(cotangent[i] * normed[i]) for i in group}
        d = {i: ((cotangent[i] - normed[i] * inner[i]) * inverse[i]).astype(BF16) for i in group}
        grad = {i: dot(query[i], d[i], (0, 0)) for i in group}
        for j, n in group:
            states[n, j] = state[j, n]
            target[n][:, to[j]] = normed[j, n].astype(BF16)
            d_attn[n, :, to[j]] = d[j, n]
            every[n, j] = grad[j, n].astype(BF16)
            if n == 1:
                grad_sum[j] = (grad[j, 0] + grad[j, 1]).astype(BF16)


def middle_kernel(share, qg_own, qg_other, kv_own, kv_other, weights_own, weights_other, *refs):
    weights = weights_own, weights_other
    d_attn, states, att_other = refs[:OWNERS], refs[OWNERS : 2 * OWNERS], refs[2 * OWNERS : 3 * OWNERS]
    dq_own, send, key_part, value_part = refs[3 * OWNERS :]
    causal = causal_mask(qg_own.shape[1])
    for r in range(OWNERS):
        for j in range(share):
            head, at = share_columns(r, j, share)
            to = slice(j * DH, (j + 1) * DH)
            send[0, :, at] = att_other[r][:, to]
            for n, (qg, kv) in enumerate(((qg_own, kv_own), (qg_other, kv_other))):
                d = d_attn[r][n, :, to]
                dw = jnp.where(causal, dot(d, kv[1, :, at], (1, 1)), 0.0).astype(BF16)
                d_query = (dot(dw, kv[0, :, at], (1, 0)) + dot(d, states[r][n, j], (1, 1))).astype(BF16)
                if n == 0:
                    dq_own[:, at] = d_query
                else:
                    send[1, :, at] = d_query
                key_part[n, :, at] = dot(dw, qg[0, :, at], (0, 0))
                value_part[n, :, at] = dot(weights[n][head], d, (0, 0))


def final_kernel(share, r, kv_own, kv_other, key_part, value_part, base, local, own, send):
    for j in range(share):
        _, at = share_columns(r, j, share)
        to = slice(j * DH, (j + 1) * DH)
        after = base[j].astype(F32)
        for n, (kv, out) in enumerate(((kv_own, own), (kv_other, send))):
            state = (after + local[r, n, j]).astype(BF16)
            out[0, :, to] = (key_part[n, :, at] + dot(kv[1, :, at], state, (1, 1))).astype(BF16)
            out[1, :, to] = (value_part[n, :, at] + dot(kv[0, :, at], state, (1, 0))).astype(BF16)


def radices(planes):
    bits, found = 1, []
    while bits < planes:
        masks = [bits, 2 * bits, 3 * bits] if 2 * bits < planes else [bits]
        found.append(masks)
        bits *= 4
    return found


def scan(sums, every, reverse, work, later):
    count = lax.axis_size(AXES[0]) * lax.axis_size(AXES[1])
    _, near, _ = pair_bit()
    received = [sums[0]] + [None] * (OWNERS - 1)
    for r in OUT:
        received[r] = swap(sums[r], owner_xor(r))
    direct = swap(every, near)
    shape = jax.ShapeDtypeStruct(sums[0].shape, BF16)
    (total,) = call(sum_kernel, received, [shape], grant=4)
    total, later = lax.optimization_barrier((total, later)) if reverse else (total, later)
    others, steps = [], []
    levels = radices(count // PLANE)
    for level, masks in enumerate(levels):
        got = [swap(total, mask * PLANE) for mask in reversed(masks)]
        others, steps = others + got, steps + masks[::-1]
        if level + 1 < len(levels):
            (total,) = call(sum_kernel, [total, *got], [shape], grant=4)
    done = work(*later)
    others, done = lax.optimization_barrier((others, done))
    mine, across = call(functools.partial(base_kernel, reverse, steps), [*received, *others], [shape] * 2, grant=4)
    (local,) = call(functools.partial(local_kernel, reverse), [every, direct], [jax.ShapeDtypeStruct(every.shape, F32)])
    bases = [mine] + [None] * (OWNERS - 1)
    for r in ARRIVAL[1:]:
        bases[r] = swap(across if r & 2 else mine, owner_xor(r))
    return bases, local, done


def body(queries, key_rows, value_rows, grad_output):
    rows, width = queries.shape
    half = width // 2
    heads = half // DH
    share = heads // OWNERS
    count = lax.axis_size(AXES[0]) * lax.axis_size(AXES[1])
    assert count % PLANE == 0 and count & (count - 1) == 0 and heads % OWNERS == 0
    pair = pair_bit()[0]
    one = 4 * rows * half * DH
    of = jax.ShapeDtypeStruct
    flat, flat_two, wide = of((rows, half), BF16), of((2, rows, half), BF16), of((2, rows, half), F32)
    full = of((rows, width), BF16)
    part, part_two = of((rows, share * DH), BF16), of((2, rows, share * DH), BF16)
    state, state_two = of((share, DH, DH), BF16), of((2, share, DH, DH), BF16)
    state_all = of((OWNERS, 2, share, DH, DH), BF16)
    sems = pltpu.SemaphoreType.DMA

    kv_send, kv_own = (
        call(
            functools.partial(split_kernel, partner),
            [key_rows, value_rows],
            [flat_two],
            hbm_in=True,
            scratch=[sems((2, 4))],
            grant=53,
        )[0]
        for partner in (True, False)
    )
    kv_other = swap(kv_send, pair)
    *sums, every = call(
        functools.partial(states_kernel, share), [kv_own, kv_other], [state] * OWNERS + [state_all], one
    )
    queries, grad_output, *sums = lax.optimization_barrier((queries, grad_output, *sums))
    qg_send, qg_own = (
        call(
            functools.partial(split_kernel, partner),
            [queries, grad_output],
            [flat_two],
            hbm_in=True,
            scratch=[sems((2, 1))],
        )[0]
        for partner in (True, False)
    )
    qg_other = swap(qg_send, pair)

    def within_work(*operands):
        found = []
        for n in range(2):
            found += call(
                functools.partial(within_kernel, heads),
                operands[2 * n : 2 * n + 2],
                [of((heads, rows, rows), BF16), of((rows, half), F32)],
                one,
            )
        return found

    bases, local, (weights_own, within_own, weights_other, within_other) = scan(
        sums, every, False, within_work, (qg_own, kv_own, qg_other, kv_other)
    )
    results = [None] * OWNERS
    for r in BACK:
        results[r] = call(
            functools.partial(forward_kernel, share, r),
            [qg_own, qg_other, within_own, within_other, bases[r], local],
            [state, part, part, part_two, state_two, state_two],
            2 * one // OWNERS,
        )
    grad_sums, att_own, att_other, d_attn, states, grad_every = zip(*results)
    (every,) = call(pack_kernel, grad_every, [state_all])

    def middle_work(*operands):
        return call(functools.partial(middle_kernel, share), operands, [flat, flat_two, wide, wide], 5 * one)

    bases, local, (dq_own, send, key_part, value_part) = scan(
        grad_sums,
        every,
        True,
        middle_work,
        (qg_own, qg_other, kv_own, kv_other, weights_own, weights_other, *d_attn, *states, *att_other),
    )
    swapped = swap(send, pair)
    attended, grad_queries = call(
        join_own_kernel, [*att_own, dq_own], [full] * 2, hbm_out=True, scratch=[sems((OWNERS + 1,))]
    )
    own, received, send = [None] * OWNERS, [None] * OWNERS, None
    for r in ARRIVAL:
        if send is not None:
            bases[r], send = lax.optimization_barrier((bases[r], send))
            received[last] = swap(send, pair)
        last = r
        own[r], send = call(
            functools.partial(final_kernel, share, r),
            [kv_own, kv_other, key_part, value_part, bases[r], local],
            [part_two] * 2,
            2 * one // OWNERS,
        )
    received[last] = swap(send, pair)
    early = 1
    attended, grad_queries, grad_keys, grad_values = call(
        functools.partial(join_most_kernel, early),
        [attended, grad_queries, swapped, *own, *(received[r] for r in ARRIVAL[:early])],
        [full] * 4,
        hbm_out=True,
        scratch=[sems((1 + OWNERS + early, 2))],
        alias=2,
    )
    grad_keys, grad_values = call(
        functools.partial(join_rest_kernel, early),
        [grad_keys, grad_values, *(received[r] for r in ARRIVAL[early:])],
        [full] * 2,
        hbm_out=True,
        scratch=[sems((OWNERS - early, 2))],
        alias=2,
    )
    return (attended, grad_queries, grad_keys, grad_values)


def solution(mesh):
    spec = P(AXES, None)

    return jax.shard_map(body, mesh=mesh, in_specs=(spec,) * 4, out_specs=(spec,) * 4, check_vma=False)
```

```python
import functools

import jax
import jax.numpy as jnp
from jax import lax
from jax.experimental import pallas as pl
from jax.experimental.pallas import tpu as pltpu
from jax.sharding import PartitionSpec as P


DH = 128
AXES = ("context", "tensor")
PLANE = 8
GROUP = 4
OWNERS = 4
OUT = (3, 1, 2)
BACK = (0, 1, 3, 2)
ARRIVAL = (0, 3, 1, 2)
TOGETHER = 3

eps = 1e-06

F32 = jnp.float32
BF16 = jnp.bfloat16


def dot(a, b, contract):
    return lax.dot_general(a, b, ((contract[:1], contract[1:]), ((), ())), preferred_element_type=F32)


def pair_bit():
    pair = lax.axis_size(AXES[1]) if lax.axis_size(AXES[1]) < GROUP else 1
    return pair, (GROUP - 1) ^ pair, GROUP


def here():
    return lax.axis_index(AXES[0]) * lax.axis_size(AXES[1]) + lax.axis_index(AXES[1])


def has(bit):
    return jnp.bitwise_and(here(), bit) > 0


def owner_xor(r):
    _, near, far = pair_bit()
    return (near if r & 1 else 0) ^ (far if r & 2 else 0)


def owner():
    _, near, far = pair_bit()
    return has(near).astype(jnp.int32) + 2 * has(far).astype(jnp.int32)


def swap(x, bits):
    count = lax.axis_size(AXES[0]) * lax.axis_size(AXES[1])
    return lax.ppermute(x, AXES, [(i, i ^ bits) for i in range(count)])


def call(kernel, inputs, outs, flops=0, hbm_in=False, hbm_out=False, scratch=(), grant=16, alias=0):
    space_in = pl.BlockSpec(memory_space=pl.ANY if hbm_in else pltpu.VMEM)
    space_out = pl.BlockSpec(memory_space=pl.ANY if hbm_out else pltpu.VMEM)
    moved = sum(a.size * a.dtype.itemsize for a in list(inputs) + list(outs))
    return pl.pallas_call(
        kernel,
        out_shape=list(outs),
        in_specs=[pl.BlockSpec(memory_space=pl.ANY)] * alias + [space_in] * (len(inputs) - alias),
        out_specs=[space_out] * len(outs),
        scratch_shapes=list(scratch),
        input_output_aliases={n: n for n in range(alias)},
        compiler_params=pltpu.CompilerParams(vmem_limit_bytes=grant * 1024 * 1024),
        cost_estimate=pl.CostEstimate(flops=flops, bytes_accessed=moved, transcendentals=0),
    )(*inputs)


def share_columns(r, j, share):
    head = jnp.bitwise_xor(owner(), r) * share + j
    return head, pl.ds(pl.multiple_of(head * DH, DH), DH)


def causal_mask(rows):
    return lax.broadcasted_iota(jnp.int32, (rows, rows), 0) >= lax.broadcasted_iota(jnp.int32, (rows, rows), 1)


def run_copies(copies):
    for copy in copies:
        copy.start()
    for copy in copies:
        copy.wait()


def half_columns(partner):
    mine = has(pair_bit()[0]).astype(jnp.int32)
    return 1 - mine if partner else mine


def split_kernel(partner, a, b, out, sems):
    _, rows, half = out.shape
    chunks = sems.shape[1]
    at = pl.ds(pl.multiple_of(half_columns(partner) * half, half), half)
    copies = []
    for k in range(chunks):
        take = slice(k * rows // chunks, (k + 1) * rows // chunks)
        for n, source in enumerate((a, b)):
            copies.append(pltpu.make_async_copy(source.at[take, at], out.at[n, take], sems.at[n, k]))
    run_copies(copies)


def write_half(source, target, partner, sem):
    half = source.shape[1]
    at = pl.ds(pl.multiple_of(half_columns(partner) * half, half), half)
    return pltpu.make_async_copy(source, target.at[:, at], sem)


def write_share(source, target, partner, r, sem):
    width = source.shape[1]
    start = (half_columns(partner) * OWNERS + jnp.bitwise_xor(owner(), r)) * width
    return pltpu.make_async_copy(source, target.at[:, pl.ds(pl.multiple_of(start, width), width)], sem)


def join_own_kernel(*refs):
    att_own, dq_own, (attended, grad_queries), sems = refs[:OWNERS], refs[OWNERS], refs[OWNERS + 1 : -1], refs[-1]
    copies = [write_half(dq_own, grad_queries, False, sems.at[OWNERS])]
    copies += [write_share(att_own[r], attended, False, r, sems.at[r]) for r in range(OWNERS)]
    run_copies(copies)


def join_most_kernel(count, *refs):
    swapped, own = refs[2], refs[3 : 3 + OWNERS]
    received, outs, sems = refs[3 + OWNERS : 3 + OWNERS + count], refs[3 + OWNERS + count : -1], refs[-1]
    copies = []
    for n in range(2):
        copies.append(write_half(swapped.at[n], outs[n], True, sems.at[0, n]))
        for r in range(OWNERS):
            copies.append(write_share(own[r].at[n], outs[2 + n], False, r, sems.at[1 + r, n]))
        for k, r in enumerate(ARRIVAL[:count]):
            copies.append(write_share(received[k].at[n], outs[2 + n], True, r, sems.at[1 + OWNERS + k, n]))
    run_copies(copies)


def join_rest_kernel(where, *refs):
    received, outs, sems = refs[2:-3], refs[-3:-1], refs[-1]
    copies = []
    for r, (k, n) in enumerate(where):
        copies += [write_share(received[k].at[n, m], outs[m], True, r, sems.at[r, m]) for m in range(2)]
    run_copies(copies)


def states_kernel(share, own, other, *outs):
    sums, every = outs[:OWNERS], outs[OWNERS]
    for r in range(OWNERS):
        for j in range(share):
            _, at = share_columns(r, j, share)
            first = dot(own[0, :, at], own[1, :, at], (0, 0))
            second = dot(other[0, :, at], other[1, :, at], (0, 0))
            every[r, 0, j] = first.astype(BF16)
            every[r, 1, j] = second.astype(BF16)
            sums[r][j] = (first + second).astype(BF16)


def sum_kernel(*refs):
    for j in range(refs[0].shape[0]):
        refs[-1][j] = sum(ref[j].astype(F32) for ref in refs[:-1]).astype(BF16)


def pack_kernel(*refs):
    for r in range(OWNERS):
        refs[-1][r] = refs[r][...]


def base_kernel(reverse, steps, *refs):
    count = len(steps)
    parts, others, (mine, across) = refs[:OWNERS], refs[OWNERS : OWNERS + count], refs[OWNERS + count :]
    late = has(pair_bit()[2])
    counts_far = jnp.logical_not(late) if reverse else late
    plane = here() // PLANE
    for j in range(mine.shape[0]):
        base = jnp.zeros(mine.shape[1:], F32)
        for other, step in zip(others, steps):
            source = jnp.bitwise_xor(plane, step)
            keep = source > plane if reverse else source < plane
            base = base + jnp.where(keep, other[j].astype(F32), 0.0)
        same = parts[0][j].astype(F32) + parts[1][j].astype(F32)
        far = parts[2][j].astype(F32) + parts[3][j].astype(F32)
        mine[j] = (base + jnp.where(counts_far, far, 0.0)).astype(BF16)
        across[j] = (base + jnp.where(counts_far, 0.0, same)).astype(BF16)


def local_kernel(reverse, every, direct, out):
    pair, near, _ = pair_bit()
    place = jnp.bitwise_and(here(), GROUP - 1)
    for r in range(OWNERS):
        for j in range(every.shape[2]):
            sources = [(0, every[r, 0, j]), (pair, every[r, 1, j])]
            sources += [(near, direct[r ^ 1, 0, j]), (near ^ pair, direct[r ^ 1, 1, j])]
            sources = [(mask, state.astype(F32)) for mask, state in sources]
            for n, target in enumerate((0, pair)):
                to = jnp.bitwise_xor(place, target)
                total = jnp.zeros(every.shape[3:], F32)
                for mask, state in sources:
                    if mask != target:
                        source = jnp.bitwise_xor(place, mask)
                        total = total + jnp.where(source > to if reverse else source < to, state, 0.0)
                out[r, n, j] = total


def within_kernel(heads, qg, kv, weights, attn):
    causal = causal_mask(qg.shape[1])
    for h in range(heads):
        at = slice(h * DH, (h + 1) * DH)
        w = jnp.where(causal, dot(qg[0, :, at], kv[0, :, at], (1, 1)), 0.0).astype(BF16)
        weights[h] = w
        attn[:, at] = dot(w, kv[1, :, at], (1, 0))


def forward_kernel(
    share, r, qg_own, qg_other, within_own, within_other, base, local, grad_sum, att_own, att_other, d_attn, states, every
):
    source, within, target = (qg_own, qg_other), (within_own, within_other), (att_own, att_other)

    def mean(x):
        return jnp.mean(x, axis=1, keepdims=True)

    for group in [[(j, n) for j in range(share) for n in range(2)]]:
        at = {j: share_columns(r, j, share)[1] for j, _ in group}
        to = {j: slice(j * DH, (j + 1) * DH) for j, _ in group}
        state = {(j, n): (base[j].astype(F32) + local[r, n, j]).astype(BF16) for j, n in group}
        query = {(j, n): source[n][0, :, at[j]] for j, n in group}
        attn = {(j, n): within[n][:, at[j]] + dot(query[j, n], state[j, n], (1, 0)) for j, n in group}
        inverse = {i: lax.rsqrt(mean(attn[i] * attn[i]) + eps) for i in group}
        normed = {i: attn[i] * inverse[i] for i in group}
        cotangent = {(j, n): source[n][1, :, at[j]].astype(F32) for j, n in group}
        inner = {i: mean(cotangent[i] * normed[i]) for i in group}
        d = {i: ((cotangent[i] - normed[i] * inner[i]) * inverse[i]).astype(BF16) for i in group}
        grad = {i: dot(query[i], d[i], (0, 0)) for i in group}
        for j, n in group:
            states[n, j] = state[j, n]
            target[n][:, to[j]] = normed[j, n].astype(BF16)
            d_attn[n, :, to[j]] = d[j, n]
            every[n, j] = grad[j, n].astype(BF16)
            if n == 1:
                grad_sum[j] = (grad[j, 0] + grad[j, 1]).astype(BF16)


def middle_kernel(share, qg_own, qg_other, kv_own, kv_other, weights_own, weights_other, *refs):
    weights = weights_own, weights_other
    d_attn, states, att_other = refs[:OWNERS], refs[OWNERS : 2 * OWNERS], refs[2 * OWNERS : 3 * OWNERS]
    dq_own, send, key_part, value_part = refs[3 * OWNERS :]
    causal = causal_mask(qg_own.shape[1])
    for r in range(OWNERS):
        for j in range(share):
            head, at = share_columns(r, j, share)
            to = slice(j * DH, (j + 1) * DH)
            send[0, :, at] = att_other[r][:, to]
            for n, (qg, kv) in enumerate(((qg_own, kv_own), (qg_other, kv_other))):
                d = d_attn[r][n, :, to]
                dw = jnp.where(causal, dot(d, kv[1, :, at], (1, 1)), 0.0).astype(BF16)
                d_query = (dot(dw, kv[0, :, at], (1, 0)) + dot(d, states[r][n, j], (1, 1))).astype(BF16)
                if n == 0:
                    dq_own[:, at] = d_query
                else:
                    send[1, :, at] = d_query
                key_part[n, :, at] = dot(dw, qg[0, :, at], (0, 0))
                value_part[n, :, at] = dot(weights[n][head], d, (0, 0))


def final_kernel(share, r, kv_own, kv_other, key_part, value_part, base, local, *refs):
    earlier, (own, sends) = refs[:-2], refs[-2:]
    for k, ref in enumerate(earlier):
        sends[k] = ref[0]
    send = sends.at[len(earlier)]
    for j in range(share):
        _, at = share_columns(r, j, share)
        to = slice(j * DH, (j + 1) * DH)
        after = base[j].astype(F32)
        for n, (kv, out) in enumerate(((kv_own, own), (kv_other, send))):
            state = (after + local[r, n, j]).astype(BF16)
            out[0, :, to] = (key_part[n, :, at] + dot(kv[1, :, at], state, (1, 1))).astype(BF16)
            out[1, :, to] = (value_part[n, :, at] + dot(kv[0, :, at], state, (1, 0))).astype(BF16)


def radices(planes):
    bits, found = 1, []
    while bits < planes:
        masks = [bits, 2 * bits, 3 * bits] if 2 * bits < planes else [bits]
        found.append(masks)
        bits *= 4
    return found


def scan(sums, every, reverse, work, later):
    count = lax.axis_size(AXES[0]) * lax.axis_size(AXES[1])
    _, near, _ = pair_bit()
    received = [sums[0]] + [None] * (OWNERS - 1)
    for r in OUT:
        received[r] = swap(sums[r], owner_xor(r))
    direct = swap(every, near)
    shape = jax.ShapeDtypeStruct(sums[0].shape, BF16)
    (total,) = call(sum_kernel, received, [shape], grant=4)
    total, later = lax.optimization_barrier((total, later)) if reverse else (total, later)
    others, steps = [], []
    levels = radices(count // PLANE)
    for level, masks in enumerate(levels):
        got = [swap(total, mask * PLANE) for mask in reversed(masks)]
        others, steps = others + got, steps + masks[::-1]
        if level + 1 < len(levels):
            (total,) = call(sum_kernel, [total, *got], [shape], grant=4)
    done = work(*later)
    others, done = lax.optimization_barrier((others, done))
    mine, across = call(functools.partial(base_kernel, reverse, steps), [*received, *others], [shape] * 2, grant=4)
    (local,) = call(functools.partial(local_kernel, reverse), [every, direct], [jax.ShapeDtypeStruct(every.shape, F32)])
    bases = [mine] + [None] * (OWNERS - 1)
    for r in ARRIVAL[1:]:
        bases[r] = swap(across if r & 2 else mine, owner_xor(r))
    return bases, local, done


def body(queries, key_rows, value_rows, grad_output):
    rows, width = queries.shape
    half = width // 2
    heads = half // DH
    share = heads // OWNERS
    count = lax.axis_size(AXES[0]) * lax.axis_size(AXES[1])
    assert count % PLANE == 0 and count & (count - 1) == 0 and heads % OWNERS == 0
    pair = pair_bit()[0]
    one = 4 * rows * half * DH
    of = jax.ShapeDtypeStruct
    flat, flat_two, wide = of((rows, half), BF16), of((2, rows, half), BF16), of((2, rows, half), F32)
    full = of((rows, width), BF16)
    part, part_two = of((rows, share * DH), BF16), of((2, rows, share * DH), BF16)
    state, state_two = of((share, DH, DH), BF16), of((2, share, DH, DH), BF16)
    state_all = of((OWNERS, 2, share, DH, DH), BF16)
    sems = pltpu.SemaphoreType.DMA

    kv_send, kv_own = (
        call(
            functools.partial(split_kernel, partner),
            [key_rows, value_rows],
            [flat_two],
            hbm_in=True,
            scratch=[sems((2, 1))],
            grant=53,
        )[0]
        for partner in (True, False)
    )
    kv_other = swap(kv_send, pair)
    *sums, every = call(
        functools.partial(states_kernel, share), [kv_own, kv_other], [state] * OWNERS + [state_all], one
    )
    queries, grad_output, *sums = lax.optimization_barrier((queries, grad_output, *sums))
    qg_send, qg_own = (
        call(
            functools.partial(split_kernel, partner),
            [queries, grad_output],
            [flat_two],
            hbm_in=True,
            scratch=[sems((2, 1))],
        )[0]
        for partner in (True, False)
    )
    qg_other = swap(qg_send, pair)

    def within_work(*operands):
        found = []
        for n in range(2):
            found += call(
                functools.partial(within_kernel, heads),
                operands[2 * n : 2 * n + 2],
                [of((heads, rows, rows), BF16), of((rows, half), F32)],
                one,
            )
        return found

    bases, local, (weights_own, within_own, weights_other, within_other) = scan(
        sums, every, False, within_work, (qg_own, kv_own, qg_other, kv_other)
    )
    results = [None] * OWNERS
    for r in BACK:
        results[r] = call(
            functools.partial(forward_kernel, share, r),
            [qg_own, qg_other, within_own, within_other, bases[r], local],
            [state, part, part, part_two, state_two, state_two],
            2 * one // OWNERS,
        )
    grad_sums, att_own, att_other, d_attn, states, grad_every = zip(*results)
    (every,) = call(pack_kernel, grad_every, [state_all])

    def middle_work(*operands):
        return call(functools.partial(middle_kernel, share), operands, [flat, flat_two, wide, wide], 5 * one)

    bases, local, (dq_own, send, key_part, value_part) = scan(
        grad_sums,
        every,
        True,
        middle_work,
        (qg_own, qg_other, kv_own, kv_other, weights_own, weights_other, *d_attn, *states, *att_other),
    )
    swapped = swap(send, pair)
    attended, grad_queries = call(
        join_own_kernel, [*att_own, dq_own], [full] * 2, hbm_out=True, scratch=[sems((OWNERS + 1,))]
    )
    own, received, waiting = [None] * OWNERS, [None] * OWNERS, []
    for k, r in enumerate(ARRIVAL):
        whole = k + 1 >= TOGETHER
        earlier = waiting if whole else []
        own[r], send = call(
            functools.partial(final_kernel, share, r),
            [kv_own, kv_other, key_part, value_part, bases[r], local, *earlier],
            [part_two, of((1 + len(earlier), *part_two.shape), BF16)],
            2 * one // OWNERS,
        )
        if not whole:
            waiting.append(send)
            continue
        if k + 1 < OWNERS:
            bases[ARRIVAL[k + 1]], send = lax.optimization_barrier((bases[ARRIVAL[k + 1]], send))
        got = swap(send, pair)
        for n in range(1 + len(earlier)):
            received[ARRIVAL[k - len(earlier) + n]] = (got, n)
        waiting = []
    attended, grad_queries, grad_keys, grad_values = call(
        functools.partial(join_most_kernel, 0),
        [attended, grad_queries, swapped, *own],
        [full] * 4,
        hbm_out=True,
        scratch=[sems((1 + OWNERS, 2))],
        alias=2,
    )
    sources = []
    for got, _ in received:
        if not any(got is source for source in sources):
            sources.append(got)
    where = [next((k, n) for k, source in enumerate(sources) if source is got) for got, n in received]
    grad_keys, grad_values = call(
        functools.partial(join_rest_kernel, where),
        [grad_keys, grad_values, *sources],
        [full] * 2,
        hbm_out=True,
        scratch=[sems((OWNERS, 2))],
        alias=2,
    )
    return (attended, grad_queries, grad_keys, grad_values)


def solution(mesh):
    spec = P(AXES, None)

    return jax.shard_map(body, mesh=mesh, in_specs=(spec,) * 4, out_specs=(spec,) * 4, check_vma=False)
```
